32 devices in a mesh: tok: 16 (over z, x, core), col: 2 (over y).
Axes of the slice: x: 2, y: 2, z: 4, core: 2. Of those that a mesh axis runs over, the one named last changes fastest.
Arguments:
- tokens: bfloat16 [12288, 2048], P('tok', 'col'), may hold values from -6 to 6
- cotangent: bfloat16 [12288, 2048], P('tok', 'col'), may hold values from -6 to 6
- query_weight: bfloat16 [2048, 2048], P(None, 'col'), may hold values from -1 to 1
- slot_keys: bfloat16 [16384, 2048], P('tok', 'col'), may hold values from -64 to 64
- values: float32 [16384, 2048], P('tok', 'col'), may hold values from -6 to 6
- momentum: float32 [16384, 2048], P('tok', 'col'), may hold values from -0.3 to 0.3
- page_ids: int32 [192, 4], P('tok'), may hold values from 0 to 127, as said below
- last_step: int32 [128], P('tok'), may hold values from 0 to 63
- decay_rate: float32 [2048], P('col'), may hold values from 0.004 to 0.08
- gate_weight: bfloat16 [2048, 2048], P(None, 'col'), may hold values from -0.125 to 0.125
- out_weight: bfloat16 [2048, 2048], P('col'), may hold values from -0.1875 to 0.1875
Outputs:
- layer_out: bfloat16 [12288, 2048], P('tok', 'col')
- new_values: float32 [16384, 2048], P('tok', 'col')
- new_momentum: float32 [16384, 2048], P('tok', 'col')
The draws below stay inside these ranges and needn't reach their ends.
Inputs may be any that keep to these rules, and one draw needn't show every extreme that they name: `page_ids`: page p belongs to owner group p // 8. Among the 48 pages listed by the blocks of one index of tok, counted with repeats, at most 4 belong to any one owner group, and one owner group gets exactly 4 from every index of tok. A block may list a page more than once.
All inputs are finite; a program needn't handle non-finite values.
Results may differ from the reference program's by a relative error of at most 0.014.
Values may be sent and summed in bfloat16 or wider, within the bound.
No kernel may reach another device: no remote copies, remote signals or barrier semaphores. Data moves between devices by JAX's collectives and lax.ppermute only.
A program may use at most 128 MiB of HBM per device.

```python
import math
import jax
import jax.numpy as jnp
from jax import lax

D = 2048
KW = 2048
PAGE = 128
PICKS = 4
BLK = 64
STEP = 64
NB = 12
PAGES_DEV = 8
TOKENS = 12288
NBLOCKS = 192
PAGES = 128
SLOTS = 16384
CAP = 4
N_COL = 2


def page_table(key):
    base_key = jax.random.fold_in(key, 101)
    sources = PAGES // PAGES_DEV
    slots_all = sources * CAP
    skipped = max(1, PAGES_DEV // 4)
    usable = PAGES_DEV - skipped
    hot_owner = jax.random.randint(jax.random.fold_in(base_key, 1), (), 0, sources)
    owner_pool = (jnp.arange(slots_all) // CAP).astype(jnp.int32)

    def group_order(group):
        return jax.random.permutation(jax.random.fold_in(base_key, group + 5000), PAGES_DEV).astype(jnp.int32)
    orders = jax.vmap(group_order)(jnp.arange(sources))

    def one_source(source):
        source_key = jax.random.fold_in(base_key, source + 7)
        shuffled = jax.random.permutation(jax.random.fold_in(source_key, 1), slots_all).astype(jnp.int32)
        priority = jnp.where(owner_pool == hot_owner, 0, 1) * slots_all + shuffled
        ordering = jnp.argsort(priority, stable=True)
        chosen = owner_pool[ordering][:PICKS * NB]
        chosen = jax.random.permutation(jax.random.fold_in(source_key, 2), chosen)
        within = jax.random.randint(jax.random.fold_in(source_key, 3), (PICKS * NB,), 0, usable)
        in_group = orders[chosen, within]
        return (chosen * PAGES_DEV + in_group).reshape(NB, PICKS)
    return jax.vmap(one_source)(jnp.arange(sources)).reshape(NB * sources, PICKS).astype(jnp.int32)


def token_table(key):
    return jnp.clip(jax.random.normal(jax.random.fold_in(key, 202), (TOKENS, D), jnp.float32), -6.0, 6.0)


def query_table(key):
    return jnp.clip(jax.random.normal(jax.random.fold_in(key, 303), (D, KW), jnp.float32), -6.0, 6.0) / math.sqrt(D)


def draw_tokens(key, part):
    return token_table(key).astype(jnp.bfloat16)


def draw_query_weight(key, part):
    return query_table(key).astype(jnp.bfloat16)


def draw_page_ids(key, part):
    return page_table(key)


def draw_slot_keys(key, part):
    drawn = jnp.clip(jax.random.normal(jax.random.fold_in(key, 404), (SLOTS, KW), jnp.float32), -6.0, 6.0)
    return drawn.astype(jnp.bfloat16)


def with_ends(values, rng, low, largest):
    dims = values.shape
    spot = [jax.random.randint(jax.random.fold_in(rng, axis), (), 0, dims[axis]) for axis in range(len(dims))]
    values = values.at[tuple(spot)].set(low)
    longest = dims.index(max(dims))
    spot[longest] = (spot[longest] + 1) % dims[longest]
    return values.at[tuple(spot)].set(largest)


def raised(values, stream_key, source, target, parts, factor):
    def block_of(position):
        return (jnp.arange(values.shape[position]) // (values.shape[position] // parts)).reshape((-1,) + (1,) * (values.ndim - 1 - position))

    first = jax.random.permutation(stream_key, parts)[block_of(target)]
    far = (block_of(target) + parts // 2) % parts
    return jnp.where((block_of(source) == first) | (block_of(source) == far), factor * values, values)


def steps_of(own_key, extent, pieces, low, largest):
    level, own = 1.0, jax.random.fold_in(own_key, 6)
    for dim, parts in pieces:
        draws = jnp.exp(jax.random.uniform(jax.random.fold_in(own, dim), (parts,), jnp.float32, low / len(pieces), largest / len(pieces)))
        level = level * jnp.repeat(draws, extent[dim] // parts).reshape([-1 if axis == dim else 1 for axis in range(len(extent))])
    return level


def noise(stream_key, shape, scale, bound, cuts=(), kind=jnp.bfloat16):
    loudness = steps_of(stream_key, shape, cuts, -0.22, 0.18) if cuts else 1.0
    result = jax.random.normal(stream_key, shape, jnp.float32) * scale * loudness
    return jnp.minimum(jnp.maximum(result, -bound), bound).astype(kind)


def noise_with(key, dims, scale, most, split, heavy, dtype=jnp.bfloat16):
    values = scale * jax.random.normal(key, dims, jnp.float32)
    if split:
        values = values * steps_of(key, dims, split, -0.22, 0.18)
    return jnp.clip(raised(values, jax.random.fold_in(key, 3), *heavy), -most, most).astype(dtype)


def setup_inputs(seed: int = 0) -> dict:
    streams_of = jax.random.split(jax.random.key(seed), 12)
    return {
        "tokens": draw_tokens(jax.random.fold_in(streams_of[11], 71), 0),
        "cotangent": noise(streams_of[1], (TOKENS, D), 1.0, 6.0, ((0, 16), (1, 2))),
        "query_weight": draw_query_weight(jax.random.fold_in(streams_of[11], 71), 0),
        "slot_keys": draw_slot_keys(jax.random.fold_in(streams_of[11], 71), 0),
        "values": noise(streams_of[4], (SLOTS, D), 1.0, 6.0, ((0, 16), (1, 2)), jnp.float32),
        "momentum": noise(streams_of[5], (SLOTS, D), 0.05, 0.3, ((0, 16), (1, 2)), jnp.float32),
        "page_ids": draw_page_ids(jax.random.fold_in(streams_of[11], 71), 0),
        "last_step": with_ends(jax.random.randint(streams_of[7], (PAGES,), 0, STEP), jax.random.fold_in(streams_of[7], 1), 0, STEP - 1).astype(jnp.int32),
        "decay_rate": jnp.clip(jnp.exp(math.log(0.08) - 2.9957322 * jax.random.uniform(streams_of[8], (D,), jnp.float32) ** steps_of(streams_of[8], (D,), ((0, 2),), -0.2, 0.2)), 0.004, 0.08),
        "gate_weight": noise(streams_of[9], (D, D), D ** -0.5, 0.125, ((1, 2),)),
        "out_weight": noise_with(streams_of[10], (D, D), D ** -0.5, 0.1875, ((0, 2),), (0, 1, 2, 2.0)),
    }


MOMENTUM_RATE = 0.9
LEARN_RATE = 1.0


def reference(tokens, cotangent, query_weight, slot_keys, values, momentum, page_ids, last_step, decay_rate, gate_weight, out_weight):
    elapsed = (STEP - last_step).astype(jnp.float32)
    factor = jnp.exp(-elapsed[:, None] * decay_rate[None, :])
    stored = values.reshape(PAGES, PAGE, D)
    decayed = (stored * factor[:, None, :]).astype(jnp.bfloat16)
    key_pages = slot_keys.reshape(PAGES, PAGE, KW)
    queries = jnp.dot(tokens, query_weight, preferred_element_type=jnp.float32).astype(jnp.bfloat16)
    query_blocks = queries.reshape(NBLOCKS, BLK, KW)

    def lookup(block_args):
        block_queries, listed = block_args
        block_keys = key_pages[listed].reshape(PICKS * PAGE, KW)
        block_values = decayed[listed].reshape(PICKS * PAGE, D)
        scores = jnp.dot(block_queries, block_keys.T, preferred_element_type=jnp.float32) * (KW ** -0.5)
        weights = jax.nn.softmax(scores, axis=-1).astype(jnp.bfloat16)
        return weights, jnp.dot(weights, block_values, preferred_element_type=jnp.float32)

    weights, memory = lax.map(lookup, (query_blocks, page_ids))
    memory = memory.reshape(TOKENS, D)
    gate_logits = jnp.dot(tokens, gate_weight, preferred_element_type=jnp.float32)
    activation = jax.nn.silu(gate_logits)
    gated_memory = (memory * activation).astype(jnp.bfloat16)
    shard_width = D // N_COL

    def add_shard(shard_index, running):
        first_col = (shard_index * shard_width).astype(jnp.int32)
        gated_piece = lax.dynamic_slice_in_dim(gated_memory, first_col, shard_width, 1)
        weight_rows = lax.dynamic_slice_in_dim(out_weight, first_col, shard_width, 0)
        partial_value = jnp.dot(gated_piece, weight_rows, preferred_element_type=jnp.float32).astype(jnp.bfloat16)
        partial_value = lax.optimization_barrier(partial_value)
        return running + partial_value.astype(jnp.float32)

    layer_out = lax.fori_loop(0, N_COL, add_shard, jnp.zeros((TOKENS, D), jnp.float32)).astype(jnp.bfloat16)

    grad_gated = jnp.dot(cotangent, out_weight.T, preferred_element_type=jnp.float32)
    grad_memory = (grad_gated * activation).astype(jnp.bfloat16).reshape(NBLOCKS, BLK, D)

    def accumulate(running_grad, block_args):
        block_weights, block_grad, listed = block_args
        slot_grad = jnp.dot(block_weights.T, block_grad, preferred_element_type=jnp.float32).astype(jnp.bfloat16)
        running_grad = running_grad.at[listed].add(slot_grad.astype(jnp.float32).reshape(PICKS, PAGE, D))
        return running_grad, None

    page_grad, unused = lax.scan(accumulate, jnp.zeros((PAGES, PAGE, D), jnp.float32), (weights, grad_memory, page_ids))
    touched = jnp.zeros((PAGES,), jnp.float32).at[page_ids.reshape(-1)].add(1.0) > 0.0
    touch_mask = touched[:, None, None]
    moment = momentum.reshape(PAGES, PAGE, D)
    new_momentum = jnp.where(touch_mask, MOMENTUM_RATE * moment + page_grad * factor[:, None, :], moment)
    new_values = jnp.where(touch_mask, stored * factor[:, None, :] - LEARN_RATE * new_momentum, stored)
    return layer_out, new_values.reshape(SLOTS, D), new_momentum.reshape(SLOTS, D)
```

```python
import functools

import jax
import jax.numpy as jnp
from jax import lax
from jax.experimental import pallas as pl
from jax.experimental.pallas import tpu as pltpu
from jax.sharding import PartitionSpec as P

STEP = 64
MOMENTUM_RATE = 0.9
LEARN_RATE = 1.0
FLOOR = -1e30
BF = jnp.bfloat16
F32 = jnp.float32

ANY = pl.BlockSpec(memory_space=pl.ANY)
VM = pl.BlockSpec(memory_space=pltpu.VMEM)
SM = pl.BlockSpec(memory_space=pltpu.SMEM)


def fetch(parts, store, sems):
    copies, row = [], 0
    for at, part in enumerate(parts):
        rows = part.shape[0]
        copy = pltpu.make_async_copy(part, store.at[pl.ds(row, rows), :], sems.at[at])
        copy.start()
        copies.append(copy)
        row += rows
    return copies


def score_kernel(nq, nk, blk, page, row_tab, page_tab, live, *refs):
    q_parts, k_parts = refs[:nq], refs[nq : nq + nk]
    out, q_store, k_store, q_sem, k_sem = refs[nq + nk :]
    copies = fetch(k_parts, k_store, k_sem) + fetch(q_parts, q_store, q_sem)
    for copy in copies:
        copy.wait()

    def step(slot, carry):
        row = pl.multiple_of(row_tab[slot] * blk, blk)
        key = pl.multiple_of(page_tab[slot] * page, page)
        out[slot] = lax.dot_general(
            q_store[pl.ds(row, blk), :],
            k_store[pl.ds(key, page), :],
            (((1,), (1,)), ((), ())),
            preferred_element_type=F32,
        )
        return carry

    lax.fori_loop(0, out.shape[0], step, 0)


def memory_kernel(nv, nout, blk, page, slot_tab, page_tab, w, *refs):
    v_parts, outs = refs[:nv], refs[nv : nv + nout]
    v_store, acc, v_sem = refs[nv + nout :]
    for copy in fetch(v_parts, v_store, v_sem):
        copy.wait()
    picks = slot_tab.shape[1]
    per_out = outs[0].shape[0] // blk
    for at, out in enumerate(outs):

        def step(inner, carry):
            block = at * per_out + inner
            acc[...] = jnp.zeros_like(acc)
            for pick in range(picks):
                slot = slot_tab[block, pick]

                @pl.when(slot >= 0)
                def add():
                    first = pl.multiple_of(page_tab[slot] * page, page)
                    acc[...] += jnp.dot(
                        w[slot], v_store[pl.ds(first, page), :], preferred_element_type=F32
                    )

            out[pl.ds(pl.multiple_of(inner * blk, blk), blk), :] = acc[...].astype(out.dtype)
            return carry

        lax.fori_loop(0, per_out, step, 0)


def grad_kernel(ng, blk, page, row_tab, page_tab, live, w, *refs):
    g_parts = refs[:ng]
    out, g_store, acc, g_sem = refs[ng:]
    copies = fetch(g_parts, g_store, g_sem)
    acc[...] = jnp.zeros_like(acc)
    for copy in copies:
        copy.wait()

    def step(slot, carry):
        @pl.when(live[slot] > 0)
        def add():
            row = pl.multiple_of(row_tab[slot] * blk, blk)
            first = pl.multiple_of(page_tab[slot] * page, page)
            acc[pl.ds(first, page), :] += lax.dot_general(
                w[slot],
                g_store[pl.ds(row, blk), :],
                (((0,), (0,)), ((), ())),
                preferred_element_type=F32,
            )

        return carry

    lax.fori_loop(0, w.shape[0], step, 0)
    out[...] = acc[...].astype(out.dtype)


def per_device(
    tokens,
    cotangent,
    query_weight,
    slot_keys,
    values,
    momentum,
    page_ids,
    last_step,
    decay_rate,
    gate_weight,
    out_weight,
):
    tok_rows = tokens.shape[0]
    width = values.shape[1]
    key_width = slot_keys.shape[1]
    nblk, picks = page_ids.shape
    blk = tok_rows // nblk
    pages = last_step.shape[0]
    page = values.shape[0] // pages
    owners = lax.axis_size("tok")
    cols = lax.axis_size("col")
    me = lax.axis_index("tok")
    col = lax.axis_index("col")
    cap = max(2, picks * nblk // owners + 1)
    top = owners // 2
    group_bits = [1 << b for b in range(1, owners.bit_length() - 2)]
    sources = owners // 4

    def swap(x, bit):
        return lax.ppermute(x, "tok", [(i, i ^ bit) for i in range(owners)])

    def over(x):
        return lax.ppermute(x, "col", [(0, 1), (1, 0)])

    def gather_group(x, order):
        pieces = {0: x}
        for bit in order:
            for at in sorted(pieces):
                pieces[at | bit] = swap(pieces[at], bit)
        return [pieces[2 * at] for at in range(sources)]

    def scatter_group(pieces, order):
        pieces = {2 * at: piece for at, piece in enumerate(pieces)}
        for bit in order:
            for at in sorted(p for p in pieces if p & bit):
                sent = swap(pieces.pop(at), bit)
                kept = pieces[at ^ bit]
                total = kept.astype(F32) + sent.astype(F32)
                pieces[at ^ bit] = total if len(pieces) == 1 else total.astype(BF)
        return pieces[0]

    half = (nblk // 2) * blk

    def gather_rows(x):
        low = gather_group(x[:half], group_bits)
        high = gather_group(x[half:], group_bits[::-1])
        return [part for pair in zip(low, high) for part in pair]

    def full_width(x):
        if cols != 2:
            return lax.all_gather(x, "col", axis=1, tiled=True)
        other = over(x)
        return jnp.where(
            col == 0,
            jnp.concatenate([x, other], axis=1),
            jnp.concatenate([other, x], axis=1),
        )

    listed = page_ids
    for bit in group_bits:
        listed = jnp.concatenate([listed, swap(listed, bit)], axis=0)
    owner_rel = (listed // pages) ^ me
    hosted = (owner_rel & (owners - 1 - top - 1)) == 0
    host = jnp.where(hosted, (owner_rel & 1) + 2 * (owner_rel // top), 4)
    host_by_source = host.reshape(sources, nblk * picks)
    order = jnp.arange(nblk * picks)
    same = host_by_source[:, :, None] == host_by_source[:, None, :]
    rank = jnp.sum(same & (order[None, :] < order[:, None])[None], axis=2)
    source_at = jnp.arange(sources)[:, None]
    slot = (host_by_source * sources + source_at) * cap + rank
    nslots = 4 * sources * cap
    slot = jnp.where(hosted.reshape(sources, -1), slot, -1)
    slot_tab = slot.reshape(sources * nblk, picks).astype(jnp.int32)
    hit = slot.reshape(-1)[None, :] == jnp.arange(nslots)[:, None]
    page_at = (host * pages + listed % pages).reshape(-1)
    block_at = jnp.arange(sources * nblk * picks) // picks
    page_tab = jnp.sum(jnp.where(hit, page_at[None, :], 0), axis=1).astype(jnp.int32)
    row_tab = jnp.sum(jnp.where(hit, block_at[None, :], 0), axis=1).astype(jnp.int32)
    live = jnp.any(hit, axis=1).astype(jnp.int32)

    keys_far = swap(slot_keys, top)
    elapsed = (STEP - last_step).astype(F32)
    factor = jnp.exp(-elapsed[:, None] * decay_rate[None, :])
    stored = values.reshape(pages, page, width)
    decayed = (stored * factor[:, None, :]).astype(BF).reshape(-1, width)
    values_far = swap(decayed, top)
    key_parts = [slot_keys, swap(slot_keys, 1), keys_far, swap(keys_far, 1)]
    value_parts = [decayed, swap(decayed, 1), values_far, swap(values_far, 1)]

    token_full = full_width(tokens)
    queries = jnp.dot(token_full, query_weight, preferred_element_type=F32).astype(BF)
    query_parts = gather_rows(queries)
    gate_logits = jnp.dot(token_full, gate_weight, preferred_element_type=F32)
    activation = jax.nn.silu(gate_logits)
    cot_full = full_width(cotangent)
    grad_gated = jnp.einsum("nd,cd->nc", cot_full, out_weight, preferred_element_type=F32)
    grad_memory = (grad_gated * activation).astype(BF)
    grad_parts = gather_rows(grad_memory)

    nq = len(query_parts)
    vmem = 60 * 2**20
    scores = pl.pallas_call(
        functools.partial(score_kernel, nq, 4, blk, page),
        out_shape=jax.ShapeDtypeStruct((nslots, blk, page), F32),
        in_specs=[SM] * 3 + [ANY] * (nq + 4),
        out_specs=VM,
        scratch_shapes=[
            pltpu.VMEM((sources * tok_rows, key_width), BF),
            pltpu.VMEM((4 * pages * page, key_width), BF),
            pltpu.SemaphoreType.DMA((nq,)),
            pltpu.SemaphoreType.DMA((4,)),
        ],
        compiler_params=pltpu.CompilerParams(vmem_limit_bytes=vmem),
        name="scores",
    )(row_tab, page_tab, live, *query_parts, *key_parts)
    if cols == 2:
        scores = scores + over(scores)
    else:
        scores = lax.psum(scores, "col")
    scores = scores * ((key_width * cols) ** (-0.5))

    slot_max = jnp.max(scores, axis=2)
    slot_sum = jnp.sum(jnp.exp(scores - slot_max[:, :, None]), axis=2)
    blocks = jnp.arange(sources * nblk)
    mine = ((row_tab[None, :] == blocks[:, None]) & (live > 0)[None, :])[:, :, None]
    row_max = jnp.max(jnp.where(mine, slot_max[None], FLOOR), axis=1)
    row_sum = jnp.sum(
        jnp.where(mine, slot_sum[None] * jnp.exp(slot_max[None] - row_max[:, None]), 0.0), axis=1
    )
    stats = jnp.stack([row_max, row_sum]).reshape(2, sources, nblk, blk)
    for bit in group_bits:
        far = swap(stats, bit)
        lead = bit // 2
        far = far.reshape(2, sources // (2 * lead), 2, lead, nblk, blk)[:, :, ::-1]
        far = far.reshape(2, sources, nblk, blk)
        peak = jnp.maximum(stats[0], far[0])
        total = stats[1] * jnp.exp(stats[0] - peak) + far[1] * jnp.exp(far[0] - peak)
        stats = jnp.stack([peak, total])
    stats = stats.reshape(2, sources * nblk, blk)
    picked = jnp.sum(jnp.where(mine[None], stats[:, :, None, :], 0.0), axis=1)
    denominator = jnp.where((live > 0)[:, None], picked[1], 1.0)
    weights = jnp.where(
        (live > 0)[:, None, None],
        jnp.exp(scores - picked[0][:, :, None]) / denominator[:, :, None],
        0.0,
    ).astype(BF)

    per_host = sources * cap
    by_host = lambda x: x.reshape((2, 2, per_host) + x.shape[1:])
    wh, rh, ph, lh = (by_host(x) for x in (weights, row_tab, page_tab, live))
    w_near = wh[:, 0]
    w_far = swap(wh[:, 1], 1)
    tables = jnp.stack([rh, ph, lh])
    tab_near = tables[:, :, 0]
    tab_far = swap(tables[:, :, 1], 1)
    far_parts = [swap(part, 1) for part in grad_parts]
    local = lambda tab: tab % pages
    g_rows = jnp.concatenate([tab_near[0], tab_far[0] + sources * nblk], axis=1)
    g_pages = jnp.concatenate([local(tab_near[1]), local(tab_far[1])], axis=1)
    g_live = jnp.concatenate([tab_near[2], tab_far[2]], axis=1)
    g_weights = jnp.concatenate([w_near, w_far], axis=1)
    ng = 2 * len(grad_parts)

    def page_grads(side, dtype):
        return pl.pallas_call(
            functools.partial(grad_kernel, ng, blk, page),
            out_shape=jax.ShapeDtypeStruct((pages * page, width), dtype),
            in_specs=[SM] * 3 + [VM] + [ANY] * ng,
            out_specs=VM,
            scratch_shapes=[
                pltpu.VMEM((2 * sources * tok_rows, width), BF),
                pltpu.VMEM((pages * page, width), F32),
                pltpu.SemaphoreType.DMA((ng,)),
            ],
            compiler_params=pltpu.CompilerParams(vmem_limit_bytes=vmem),
            name="page_grads_%d" % side,
        )(g_rows[side], g_pages[side], g_live[side], g_weights[side], *grad_parts, *far_parts)

    sent_grads = swap(page_grads(1, BF), top)

    memory_parts = pl.pallas_call(
        functools.partial(memory_kernel, 4, nq, blk, page),
        out_shape=[jax.ShapeDtypeStruct((half, width), BF)] * nq,
        in_specs=[SM] * 2 + [VM] + [ANY] * 4,
        out_specs=[VM] * nq,
        scratch_shapes=[
            pltpu.VMEM((4 * pages * page, width), BF),
            pltpu.VMEM((blk, width), F32),
            pltpu.SemaphoreType.DMA((4,)),
        ],
        compiler_params=pltpu.CompilerParams(vmem_limit_bytes=vmem),
        name="memory",
    )(slot_tab, page_tab, weights, *value_parts)
    memory = jnp.concatenate(
        [
            scatter_group(memory_parts[0::2], group_bits),
            scatter_group(memory_parts[1::2], group_bits[::-1]),
        ],
        axis=0,
    )
    gated = (memory * activation).astype(BF)
    if cols == 2:
        cut = lambda at: lax.dynamic_slice_in_dim(out_weight, at * width, width, axis=1)
        far_terms = jnp.dot(gated, cut(1 - col), preferred_element_type=F32).astype(BF)
        got_terms = over(far_terms)
        near_terms = jnp.dot(gated, cut(col), preferred_element_type=F32).astype(BF)
        layer_out = (near_terms.astype(F32) + got_terms.astype(F32)).astype(BF)
    else:
        terms = jnp.dot(gated, out_weight, preferred_element_type=F32).astype(BF)
        layer_out = lax.psum_scatter(terms, "col", scatter_dimension=1, tiled=True)

    own_grads = page_grads(0, F32)
    page_hit = lambda side: jnp.sum(
        (g_live[side] > 0)[None, :] & (g_pages[side][None, :] == jnp.arange(pages)[:, None]),
        axis=1,
    ).astype(jnp.int32)
    touched = ((page_hit(0) + swap(page_hit(1), top)) > 0)[:, None, None]
    page_grad = (own_grads + sent_grads.astype(F32)).reshape(pages, page, width)
    moment = momentum.reshape(pages, page, width)
    new_momentum = jnp.where(
        touched, MOMENTUM_RATE * moment + page_grad * factor[:, None, :], moment
    )
    new_values = jnp.where(touched, stored * factor[:, None, :] - LEARN_RATE * new_momentum, stored)
    return (layer_out, new_values.reshape(-1, width), new_momentum.reshape(-1, width))


def solution(mesh):
    in_specs = (
        P("tok", "col"),
        P("tok", "col"),
        P(None, "col"),
        P("tok", "col"),
        P("tok", "col"),
        P("tok", "col"),
        P("tok", None),
        P("tok"),
        P("col"),
        P(None, "col"),
        P("col", None),
    )
    out_specs = (P("tok", "col"), P("tok", "col"), P("tok", "col"))
    return jax.shard_map(
        per_device, mesh=mesh, in_specs=in_specs, out_specs=out_specs, check_vma=False
    )
```
